32 devices in a mesh: leaf: 2 (over y), row: 4 (over x, core), col: 4 (over z).
Axes of the slice: x: 2, y: 2, z: 4, core: 2. Of those that a mesh axis runs over, the one named last changes fastest.
Arguments:
- panel: float32 [8192, 1024], P(('leaf', 'row'), 'col'), may hold values from -1.2 to 1.2
- block_mask: int32 [64, 8], P(('leaf', 'row'), 'col'), may hold values 0 or 1
- front_rest: float32 [4096, 4096], P(('leaf', 'row'), 'col'), may hold values from -6 to 6
- row_maps: int32 [8, 4], P(('leaf', 'row')), may hold values from 0 to 3, each once within a row
- col_maps: int32 [8, 12], P(('leaf', 'col')), may hold values from 0 to 11, each once within a row
Outputs:
- parent: float32 [2048, 6144], P(('leaf', 'row'), 'col')
The draws below stay inside these ranges and needn't reach their ends.
Inputs may be any that keep to these rules, and one draw needn't show every extreme that they name: `row_maps`: each row is a permutation of 0 to 3. `col_maps`: each row is a permutation of 0 to 11; only its first 8 entries are used.
All inputs are finite; a program needn't handle non-finite values. No bound on the sum of `block_mask` on one device may be relied on, other than what follows from the above.
Results may differ from the reference program's by a relative error of at most 0.0003.
Values sent between devices are 32-bit elements; how exact they have to be, the bound alone decides.
A program may use at most 64 MiB of HBM per device.

```python
import jax
import jax.numpy as jnp
import numpy as np
from jax import lax

BLK = 128
P_SIZE = 1024
MC = 4096
PC = 6144
WR = 512
WB = 4
PCB = 12
N_LEAF = 2
N_ROW = 4
N_COL = 4


def set_ends(entries, rng, low, high):
    spot = [jax.random.randint(jax.random.fold_in(rng, axis), (), 0, length) for axis, length in enumerate(entries.shape)]
    widest = entries.shape.index(max(entries.shape))
    next_to = spot[:widest] + [(spot[widest] + 1) % entries.shape[widest]] + spot[widest + 1:]
    return entries.at[tuple(spot)].set(low).at[tuple(next_to)].set(high)


def block_scale(rng, extent, split, least, high):
    def one(axis_at, blocks):
        heights = jax.random.uniform(jax.random.fold_in(jax.random.fold_in(rng, 6), axis_at), (blocks,), jnp.float32, least / len(split), high / len(split))
        return jnp.repeat(jnp.exp(heights), extent[axis_at] // blocks).reshape((-1,) + (1,) * (len(extent) - axis_at - 1))

    factor_of = one(*split[0])
    for cut in split[1:]:
        factor_of = factor_of * one(*cut)
    return factor_of


def scatter_about(own_key, shape, deviation, bound, shards=(), held_as=jnp.bfloat16):
    loudness = block_scale(own_key, shape, shards, -0.22, 0.18) if shards else 1.0
    values = jax.random.normal(own_key, shape, jnp.float32) * deviation * loudness
    return jnp.minimum(jnp.maximum(values, -bound), bound).astype(held_as)


def setup_inputs(seed: int = 0) -> dict:
    arg_keys = jax.random.split(jax.random.key(seed), 6)
    return {
        "panel": scatter_about(arg_keys[0], (N_LEAF * MC, P_SIZE), 0.18, 1.2, ((0, 8), (1, 4)), jnp.float32),
        "block_mask": set_ends((jax.random.randint(arg_keys[1], (N_LEAF * MC // BLK, P_SIZE // BLK), 0, 4) < 3).astype(jnp.int32), jax.random.fold_in(arg_keys[1], 1), 0, 1),
        "front_rest": scatter_about(arg_keys[2], (N_LEAF * N_ROW * WR, MC), 1.0, 6.0, ((0, 8), (1, 4)), jnp.float32),
        "row_maps": jax.vmap(lambda own: jax.random.permutation(own, WB))(jax.random.split(arg_keys[3], (N_LEAF * N_ROW))).reshape((N_LEAF * N_ROW, WB)).astype(jnp.int32),
        "col_maps": jax.vmap(lambda own: jax.random.permutation(own, PCB))(jax.random.split(arg_keys[4], (N_LEAF * N_COL))).reshape((N_LEAF * N_COL, PCB)).astype(jnp.int32),
    }


def reference(panel, block_mask, front_rest, row_maps, col_maps):
    halfway = N_LEAF // 2
    win_blocks = WR // BLK
    child_blocks = MC // (BLK * N_COL)
    parent_blocks = PC // (BLK * N_COL)

    def one_child(leaf):
        leaf = leaf.astype(jnp.int32)
        rows = lax.dynamic_slice_in_dim(panel, leaf * MC, MC, 0)
        flags = lax.dynamic_slice_in_dim(block_mask, leaf * (MC // BLK), MC // BLK, 0).astype(jnp.float32)
        masked = (rows.reshape(MC // BLK, BLK, P_SIZE // BLK, BLK) * flags[:, None, :, None]).reshape(MC, P_SIZE)
        window = masked.reshape(N_ROW, MC // N_ROW, P_SIZE)[:, :WR].reshape(N_ROW * WR, P_SIZE)
        front = lax.dynamic_slice_in_dim(front_rest, leaf * (N_ROW * WR), N_ROW * WR, 0)
        update = front - jnp.dot(window, masked.T, precision=lax.Precision.HIGHEST, preferred_element_type=jnp.float32)
        rmaps = lax.dynamic_slice_in_dim(row_maps, leaf * N_ROW, N_ROW, 0)
        cmaps = lax.dynamic_slice_in_dim(col_maps, leaf * N_COL, N_COL, 0)[:, :child_blocks]
        blocks = update.reshape(N_ROW, win_blocks, BLK, N_COL, child_blocks, BLK).transpose(0, 1, 3, 4, 2, 5)
        grid_rows = jnp.arange(N_ROW, dtype=jnp.int32)[:, None, None, None]
        grid_cols = jnp.arange(N_COL, dtype=jnp.int32)[None, None, :, None]
        spread = jnp.zeros((N_ROW, win_blocks, N_COL, parent_blocks, BLK, BLK), jnp.float32)
        return spread.at[grid_rows, rmaps[:, :, None, None], grid_cols, cmaps[None, None, :, :]].set(blocks)

    spread_all = lax.map(one_child, jnp.arange(N_LEAF, dtype=jnp.int32))
    partner = np.arange(N_LEAF) ^ halfway
    summed = spread_all + spread_all[partner]
    summed = summed.reshape(N_LEAF, N_ROW, 2, win_blocks // 2, N_COL, parent_blocks, BLK, BLK)
    upper = (np.arange(N_LEAF) // halfway) % 2
    kept = summed[np.arange(N_LEAF), :, upper]
    return kept.transpose(0, 1, 2, 5, 3, 4, 6).reshape(N_LEAF * N_ROW * WR // 2, PC)
```

```python
import functools

import jax
import jax.numpy as jnp
from jax import lax
from jax.experimental import pallas as pl
from jax.experimental.pallas import tpu as pltpu
from jax.sharding import PartitionSpec as P

BLK = 128
PC = 6144
F32 = jnp.float32
BF16 = jnp.bfloat16


def split(value):
    high = value.astype(BF16)
    return high, (value - high.astype(F32)).astype(BF16)


def update_kernel(
    n_leaf, n_row, n_col,
    pick_ref, p_ref, front_hbm,
    mine_ref, got_ref,
    relay, win, col, a_cat, b_cat, front, front_sorted, snd,
    win_send, win_recv, rel_send, rel_recv, s1_send, col_recv, s2_send, fwd_send,
    sib_send, sib_recv, loc_sem, self_sem,
):
    leaf, r, c = lax.axis_index("leaf"), lax.axis_index("row"), lax.axis_index("col")
    x, k = r // 2, r % 2
    sib = lax.rem(leaf + n_leaf // 2, n_leaf)
    upper = leaf // (n_leaf // 2) % 2
    win_rows, width = win.shape[1], win.shape[2]
    win_blocks = win_rows // BLK
    keep = win_blocks // 2 * BLK
    subs = col.shape[0]
    quarter = p_ref.shape[0] // n_row
    depth = n_col * width

    def remote(src, dst, ssem, rsem, row=None, column=None, other_leaf=None):
        where = {
            "leaf": leaf if other_leaf is None else other_leaf,
            "row": r if row is None else row,
            "col": c if column is None else column,
        }
        return pltpu.make_async_remote_copy(
            src_ref=src, dst_ref=dst, send_sem=ssem, recv_sem=rsem,
            device_id=where, device_id_type=pl.DeviceIdType.MESH,
        )

    x_row, pair_row = (1 - x) * 2 + k, x * 2 + 1 - k

    front_copy = pltpu.make_async_copy(front_hbm, front, loc_sem.at[0])
    front_copy.start()
    own_window = pltpu.make_async_copy(p_ref.at[pl.ds(0, win_rows)], win.at[c], loc_sem.at[1])
    own_window.start()

    barrier = pltpu.get_barrier_semaphore()

    def greet(row, column, other_leaf):
        pl.semaphore_signal(
            barrier, inc=1, device_id={"leaf": other_leaf, "row": row, "col": column},
            device_id_type=pl.DeviceIdType.MESH,
        )

    for step in range(1, n_col):
        for kk in range(2):
            greet(x * 2 + kk, lax.rem(c + step, n_col), leaf)
    greet(pair_row, c, leaf)
    greet(x_row, c, leaf)
    greet(r, c, sib)
    pl.semaphore_wait(barrier, 2 * (n_col - 1) + 3)

    def pass_window(owner, side, source):
        return remote(
            source, win.at[owner], win_send.at[side, owner], win_recv.at[owner],
            column=c + 1 if side == 0 else c - 1,
        )

    def has(side):
        return c + 1 < n_col if side == 0 else c >= 1

    for side in range(2):
        @pl.when(has(side))
        def _():
            pass_window(c, side, p_ref.at[pl.ds(0, win_rows)]).start()

    half = 2 * quarter
    to_relay = remote(
        p_ref.at[pl.ds(pl.multiple_of((1 - x) * half, half), half)], relay,
        rel_send.at[0], rel_recv.at[0], row=x_row,
    )
    to_relay.start()

    def from_left(d):
        return c - d >= 0

    def from_right(d):
        return c + d < n_col

    def take_window(d, side, forward):
        owner = c - d if side == 0 else c + d

        @pl.when(from_left(d) if side == 0 else from_right(d))
        def _():
            pass_window(owner, side, win.at[owner]).wait_recv()
            if forward:
                @pl.when(has(side))
                def _():
                    pass_window(owner, side, win.at[owner]).start()

    for d in range(1, n_col - 1):
        for side in range(2):
            take_window(d, side, True)

    to_relay.wait_recv()

    def scatter(sub, own, kk):
        target = x * 2 + k if own else (1 - x) * 2 + k
        q = x * 2 + kk
        if own:
            start = pl.multiple_of(q * quarter + sub * BLK, BLK)
            src = p_ref.at[pl.ds(start, BLK)]
        else:
            src = relay.at[pl.ds(kk * quarter + sub * BLK, BLK)]
        dst = col.at[sub, c, pl.ds(pl.multiple_of(q * BLK, BLK), BLK)]
        slot = s1_send.at[sub, int(own), kk]
        here = jnp.logical_and(target == c, k == kk)
        away = remote(src, dst, slot, col_recv.at[sub, q, c], row=q, column=target)
        stay = pltpu.make_async_copy(src, dst, self_sem.at[sub])
        return here, away, stay

    for sub in range(subs):
        for own in (True, False):
            for kk in range(2):
                here, away, stay = scatter(sub, own, kk)

                @pl.when(here)
                def _():
                    stay.start()

                @pl.when(jnp.logical_not(here))
                def _():
                    away.start()

    def slot_of(sub, q, owner):
        return col.at[sub, owner, pl.ds(pl.multiple_of(q * BLK, BLK), BLK)]

    def hand_on(sub, q, owner, ssem, row):
        part = slot_of(sub, q, owner)
        return remote(part, part, ssem, col_recv.at[sub, q, owner], row=row)

    steps = [0]
    for d in range(1, n_col):
        steps += [-d, d]

    def each(offset, run):
        owner = c + offset
        if offset == 0:
            run(owner)
        else:
            @pl.when(from_left(-offset) if offset < 0 else from_right(offset))
            def _():
                run(owner)

    def arrive(sub, q, owner):
        hand_on(sub, q, owner, s2_send.at[sub, owner, 0], pair_row).wait_recv()

    is_source = k == c % 2

    def own_piece_at(sub, offset):
        def run(owner):
            if offset == 0:
                @pl.when(is_source)
                def _():
                    pltpu.make_async_copy(
                        slot_of(sub, r, owner), slot_of(sub, r, owner), self_sem.at[sub]
                    ).wait()

                @pl.when(jnp.logical_not(is_source))
                def _():
                    arrive(sub, r, owner)
            else:
                arrive(sub, r, owner)
            hand_on(sub, r, owner, s2_send.at[sub, owner, 0], x_row).start()
            hand_on(sub, r, owner, s2_send.at[sub, owner, 1], pair_row).start()
        return run

    def forward_piece(sub):
        def run(owner):
            arrive(sub, x_row, owner)
            hand_on(sub, x_row, owner, fwd_send.at[sub, owner], pair_row).start()
        return run

    def gather(sub):
        for at, offset in enumerate(steps):
            each(offset, own_piece_at(sub, offset))
            if at:
                each(steps[at - 1], forward_piece(sub))
        each(steps[-1], forward_piece(sub))

    first_kept = upper * (win_blocks // 2)
    first_sent = (1 - upper) * (win_blocks // 2)
    parent_at = [first_sent + i for i in range(win_blocks // 2)]
    parent_at += [first_kept + i for i in range(win_blocks // 2)]

    def picked(block_of, index, lanes):
        total = None
        for j in range(win_blocks):
            term = block_of(j) * pick_ref[parent_at[index] * win_blocks + j][:, :lanes]
            total = term if total is None else total + term
        return total

    def sort_front():
        front_copy.wait()
        for i in range(win_blocks):
            front_sorted[i * BLK:(i + 1) * BLK, :] = picked(
                lambda j: front[j * BLK:(j + 1) * BLK, :], i, front.shape[1]
            )

    def build_window():
        for side in range(2):
            take_window(n_col - 1, side, False)
        own_window.wait()
        for i in range(win_blocks):
            rows = pl.ds(i * BLK, BLK)
            for owner in range(n_col):
                high, low = split(
                    picked(lambda j: win[owner, j * BLK:(j + 1) * BLK, :], i, width)
                )
                at = owner * width
                a_cat[rows, at:at + width] = high
                a_cat[rows, depth + at:depth + at + width] = high
                a_cat[rows, 2 * depth + at:2 * depth + at + width] = low

    tile = 2 * BLK
    tiles = n_row * BLK // tile

    def multiply(sub):
        for q in (pair_row, (1 - x) * 2 + 1 - k):
            for offset in steps:
                each(offset, lambda owner: arrive(sub, q, owner))
        for owner in range(n_col):
            high, low = split(col[sub, owner])
            at = owner * width
            b_cat[:, at:at + width] = high
            b_cat[:, depth + at:depth + at + width] = low
            b_cat[:, 2 * depth + at:2 * depth + at + width] = high
        for t in range(tiles):
            cols = b_cat[t * tile:(t + 1) * tile, :]
            for part in range(2):
                product = lax.dot_general(
                    a_cat[part * keep:(part + 1) * keep, :], cols,
                    (((1,), (1,)), ((), ())), preferred_element_type=F32,
                )
                into = snd if part == 0 else mine_ref
                for i in range(win_blocks // 2):
                    for b in range(2):
                        q = t * 2 + b
                        column = (q * subs + sub) * BLK
                        into[sub * n_row + q, i * BLK:(i + 1) * BLK, :] = (
                            front_sorted[part * keep + i * BLK:part * keep + (i + 1) * BLK, column:column + BLK]
                            - product[i * BLK:(i + 1) * BLK, b * BLK:(b + 1) * BLK]
                        )
            sibling(sub, t).start()

    def sibling(sub, t):
        blocks = pl.ds(sub * n_row + t * 2, 2)
        return remote(
            snd.at[blocks], got_ref.at[blocks], sib_send.at[sub, t], sib_recv.at[sub, t], other_leaf=sib
        )

    sort_front()
    gather(0)
    build_window()
    for sub in range(subs):
        multiply(sub)
        if sub + 1 < subs:
            gather(sub + 1)

    for sub in range(subs):
        for t in range(tiles):
            sibling(sub, t).wait()
    to_relay.wait_send()
    for side in range(2):
        @pl.when(has(side))
        def _():
            pass_window(c, side, p_ref.at[pl.ds(0, win_rows)]).wait_send()

        for d in range(1, n_col - 1):
            owner = c - d if side == 0 else c + d

            @pl.when(jnp.logical_and(from_left(d) if side == 0 else from_right(d), has(side)))
            def _():
                pass_window(owner, side, win.at[owner]).wait_send()
    for sub in range(subs):
        for own in (True, False):
            for kk in range(2):
                here, away, stay = scatter(sub, own, kk)

                @pl.when(jnp.logical_not(here))
                def _():
                    away.wait_send()
        for offset in steps:
            def settle(owner):
                hand_on(sub, r, owner, s2_send.at[sub, owner, 0], x_row).wait_send()
                hand_on(sub, r, owner, s2_send.at[sub, owner, 1], pair_row).wait_send()
                hand_on(sub, x_row, owner, fwd_send.at[sub, owner], pair_row).wait_send()

            each(offset, settle)


def merge_kernel(n_row, subs, blocks, own_ref, other_ref, mine_ref, got_ref, out_ref):
    out_ref[...] = jnp.zeros_like(out_ref)
    for j in range(blocks):
        at = (j % subs) * n_row + j // subs
        spot = pl.ds(pl.multiple_of(own_ref[0, j] * BLK, BLK), BLK)
        out_ref[:, spot] = mine_ref[at]
    for j in range(blocks):
        at = (j % subs) * n_row + j // subs
        spot = pl.ds(pl.multiple_of(other_ref[0, j] * BLK, BLK), BLK)
        out_ref[:, spot] = out_ref[:, spot] + got_ref[at]


def body(sizes, panel, block_mask, front_rest, row_maps, col_maps):
    n_leaf, n_row, n_col = sizes
    local_rows, width = panel.shape
    win_rows, front_cols = front_rest.shape
    keep = win_rows // 2
    blocks = front_cols // BLK
    subs = local_rows // n_row // BLK
    parent_cols = PC // n_col
    pairs = [(source, source ^ (n_leaf // 2)) for source in range(n_leaf)]
    other_cols = lax.ppermute(col_maps, "leaf", pairs)
    flags = block_mask.astype(F32)
    masked = (
        panel.reshape(local_rows // BLK, BLK, width // BLK, BLK) * flags[:, None, :, None]
    ).reshape(local_rows, width)
    win_blocks = win_rows // BLK
    pick = (row_maps == jnp.arange(win_blocks, dtype=row_maps.dtype)[:, None]).astype(F32)
    pick = jnp.broadcast_to(pick.reshape(-1, 1, 1), (win_blocks * win_blocks, 1, front_cols))
    vmem = pl.BlockSpec(memory_space=pltpu.VMEM)
    smem = pl.BlockSpec(memory_space=pltpu.SMEM)
    dma = pltpu.SemaphoreType.DMA
    part = jax.ShapeDtypeStruct((blocks, keep, BLK), F32)
    mine, got = pl.pallas_call(
        functools.partial(update_kernel, n_leaf, n_row, n_col),
        out_shape=(part, part),
        in_specs=[vmem, vmem, pl.BlockSpec(memory_space=pl.ANY)],
        out_specs=(vmem, vmem),
        scratch_shapes=[
            pltpu.VMEM((local_rows // 2, width), F32),
            pltpu.VMEM((n_col, win_rows, width), F32),
            pltpu.VMEM((subs, n_col, n_row * BLK, width), F32),
            pltpu.VMEM((win_rows, 3 * n_col * width), BF16),
            pltpu.VMEM((n_row * BLK, 3 * n_col * width), BF16),
            pltpu.VMEM((win_rows, front_cols), F32),
            pltpu.VMEM((win_rows, front_cols), F32),
            pltpu.VMEM((blocks, keep, BLK), F32),
            dma((2, n_col)), dma((n_col,)),
            dma((1,)), dma((1,)),
            dma((subs, 2, 2)), dma((subs, n_row, n_col)),
            dma((subs, n_col, 2)), dma((subs, n_col)),
            dma((subs, n_row // 2)), dma((subs, n_row // 2)),
            dma((2,)), dma((subs,)),
        ],
        compiler_params=pltpu.CompilerParams(
            collective_id=0, has_side_effects=True, vmem_limit_bytes=40 * 1024 * 1024
        ),
        name="update",
    )(pick, masked, front_rest)
    return pl.pallas_call(
        functools.partial(merge_kernel, n_row, subs, blocks),
        out_shape=jax.ShapeDtypeStruct((keep, parent_cols), F32),
        in_specs=[smem, smem, vmem, vmem],
        out_specs=vmem,
        name="merge",
    )(col_maps, other_cols, mine, got)


def solution(mesh):
    sizes = mesh.shape["leaf"], mesh.shape["row"], mesh.shape["col"]
    return jax.shard_map(
        functools.partial(body, sizes),
        mesh=mesh,
        in_specs=(
            P(("leaf", "row"), "col"),
            P(("leaf", "row"), "col"),
            P(("leaf", "row"), "col"),
            P(("leaf", "row"), None),
            P(("leaf", "col"), None),
        ),
        out_specs=P(("leaf", "row"), "col"),
        check_vma=False,
    )
```

```python
import functools

import jax
import jax.numpy as jnp
from jax import lax
from jax.experimental import pallas as pl
from jax.experimental.pallas import tpu as pltpu
from jax.sharding import PartitionSpec as P

BLK = 128
PC = 6144
F32 = jnp.float32
BF16 = jnp.bfloat16


def split(value):
    high = value.astype(BF16)
    return high, (value - high.astype(F32)).astype(BF16)


def update_kernel(
    n_leaf, n_row, n_col,
    pick_ref, p_ref, front_hbm,
    mine_ref, got_ref,
    relay, win, col, a_cat, b_cat, front, front_sorted, snd,
    win_send, win_recv, rel_send, rel_recv, s1_send, col_recv, s2_send, fwd_send,
    sib_send, sib_recv, loc_sem, self_sem,
):
    leaf, r, c = lax.axis_index("leaf"), lax.axis_index("row"), lax.axis_index("col")
    x, k = r // 2, r % 2
    sib = lax.rem(leaf + n_leaf // 2, n_leaf)
    upper = leaf // (n_leaf // 2) % 2
    keep, width = win.shape[2], win.shape[3]
    win_rows = 2 * keep
    win_blocks = win_rows // BLK
    subs = col.shape[0]
    quarter = p_ref.shape[0] // n_row
    depth = n_col * width

    def remote(src, dst, ssem, rsem, row=None, column=None, other_leaf=None):
        where = {
            "leaf": leaf if other_leaf is None else other_leaf,
            "row": r if row is None else row,
            "col": c if column is None else column,
        }
        return pltpu.make_async_remote_copy(
            src_ref=src, dst_ref=dst, send_sem=ssem, recv_sem=rsem,
            device_id=where, device_id_type=pl.DeviceIdType.MESH,
        )

    x_row, pair_row = (1 - x) * 2 + k, x * 2 + 1 - k

    front_copy = pltpu.make_async_copy(front_hbm, front, loc_sem.at[0])
    front_copy.start()
    first_kept = upper * (win_blocks // 2)
    first_sent = (1 - upper) * (win_blocks // 2)
    parent_at = [first_sent + i for i in range(win_blocks // 2)]
    parent_at += [first_kept + i for i in range(win_blocks // 2)]

    def picked(block_of, index, lanes):
        total = None
        for j in range(win_blocks):
            term = block_of(j) * pick_ref[parent_at[index] * win_blocks + j][:, :lanes]
            total = term if total is None else total + term
        return total

    for i in range(win_blocks):
        win[i * BLK // keep, c, pl.ds(i * BLK % keep, BLK), :] = picked(
            lambda j: p_ref[j * BLK:(j + 1) * BLK, :], i, p_ref.shape[1]
        )

    barrier = pltpu.get_barrier_semaphore()

    def greet(row, column, other_leaf):
        pl.semaphore_signal(
            barrier, inc=1, device_id={"leaf": other_leaf, "row": row, "col": column},
            device_id_type=pl.DeviceIdType.MESH,
        )

    for step in range(1, n_col):
        for kk in range(2):
            greet(x * 2 + kk, lax.rem(c + step, n_col), leaf)
    greet(pair_row, c, leaf)
    greet(x_row, c, leaf)
    greet(r, c, sib)
    pl.semaphore_wait(barrier, 2 * (n_col - 1) + 3)

    def pass_window(part, owner, side):
        piece = win.at[part, owner]
        return remote(
            piece, piece, win_send.at[part, side, owner], win_recv.at[part, owner],
            column=c + 1 if side == 0 else c - 1,
        )

    def has(side):
        return c + 1 < n_col if side == 0 else c >= 1

    def send_window(part):
        for side in range(2):
            @pl.when(has(side))
            def _():
                pass_window(part, c, side).start()

    send_window(0)
    half = 2 * quarter
    to_relay = remote(
        p_ref.at[pl.ds(pl.multiple_of((1 - x) * half, half), half)], relay,
        rel_send.at[0], rel_recv.at[0], row=x_row,
    )
    to_relay.start()

    def from_left(d):
        return c - d >= 0

    def from_right(d):
        return c + d < n_col

    def take_window(part, d, side, forward):
        owner = c - d if side == 0 else c + d

        @pl.when(from_left(d) if side == 0 else from_right(d))
        def _():
            pass_window(part, owner, side).wait_recv()
            if forward:
                @pl.when(has(side))
                def _():
                    pass_window(part, owner, side).start()

    def relay_window(part):
        for d in range(1, n_col - 1):
            for side in range(2):
                take_window(part, d, side, True)

    relay_window(0)

    to_relay.wait_recv()

    def scatter(sub, own, kk):
        target = x * 2 + k if own else (1 - x) * 2 + k
        q = x * 2 + kk
        if own:
            start = pl.multiple_of(q * quarter + sub * BLK, BLK)
            src = p_ref.at[pl.ds(start, BLK)]
        else:
            src = relay.at[pl.ds(kk * quarter + sub * BLK, BLK)]
        dst = col.at[sub, c, pl.ds(pl.multiple_of(q * BLK, BLK), BLK)]
        slot = s1_send.at[sub, int(own), kk]
        here = jnp.logical_and(target == c, k == kk)
        away = remote(src, dst, slot, col_recv.at[sub, q, c], row=q, column=target)
        stay = pltpu.make_async_copy(src, dst, self_sem.at[sub])
        return here, away, stay

    def at_end(own):
        target = x * 2 + k if own else (1 - x) * 2 + k
        return jnp.logical_or(target == 0, target == n_col - 1)

    def send_quarters(sub, own, kk):
        here, away, stay = scatter(sub, own, kk)

        @pl.when(here)
        def _():
            stay.start()

        @pl.when(jnp.logical_not(here))
        def _():
            away.start()

    for sub in range(subs):
        for last in (True, False):
            for own in (True, False):
                @pl.when(at_end(own) if last else jnp.logical_not(at_end(own)))
                def _():
                    for kk in range(2):
                        send_quarters(sub, own, kk)

    send_window(1)

    def slot_of(sub, q, owner):
        return col.at[sub, owner, pl.ds(pl.multiple_of(q * BLK, BLK), BLK)]

    def hand_on(sub, q, owner, ssem, row):
        part = slot_of(sub, q, owner)
        return remote(part, part, ssem, col_recv.at[sub, q, owner], row=row)

    steps = [0]
    for d in range(1, n_col):
        steps += [-d, d]

    def each(offset, run):
        owner = c + offset
        if offset == 0:
            run(owner)
        else:
            @pl.when(from_left(-offset) if offset < 0 else from_right(offset))
            def _():
                run(owner)

    def arrive(sub, q, owner):
        hand_on(sub, q, owner, s2_send.at[sub, owner, 0], pair_row).wait_recv()

    is_source = k == c % 2

    def own_piece_at(sub, offset):
        def run(owner):
            if offset == 0:
                @pl.when(is_source)
                def _():
                    pltpu.make_async_copy(
                        slot_of(sub, r, owner), slot_of(sub, r, owner), self_sem.at[sub]
                    ).wait()

                @pl.when(jnp.logical_not(is_source))
                def _():
                    arrive(sub, r, owner)
            else:
                arrive(sub, r, owner)
            hand_on(sub, r, owner, s2_send.at[sub, owner, 0], x_row).start()
            hand_on(sub, r, owner, s2_send.at[sub, owner, 1], pair_row).start()
        return run

    def forward_piece(sub):
        def run(owner):
            arrive(sub, x_row, owner)
            hand_on(sub, x_row, owner, fwd_send.at[sub, owner], pair_row).start()
        return run

    def gather(sub):
        for at, offset in enumerate(steps):
            each(offset, own_piece_at(sub, offset))
            if at:
                each(steps[at - 1], forward_piece(sub))
        each(steps[-1], forward_piece(sub))

    def sort_front():
        front_copy.wait()
        for i in range(win_blocks):
            front_sorted[i * BLK:(i + 1) * BLK, :] = picked(
                lambda j: front[j * BLK:(j + 1) * BLK, :], i, front.shape[1]
            )

    def build_window(part):
        for side in range(2):
            take_window(part, n_col - 1, side, False)
        for owner in range(n_col):
            high, low = split(win[part, owner])
            at = owner * width
            rows = slice(part * keep, (part + 1) * keep)
            a_cat[rows, at:at + width] = high
            a_cat[rows, depth + at:depth + at + width] = high
            a_cat[rows, 2 * depth + at:2 * depth + at + width] = low

    tile = 2 * BLK
    tiles = n_row * BLK // tile

    def build_columns(sub):
        for q in (pair_row, (1 - x) * 2 + 1 - k):
            for offset in steps:
                each(offset, lambda owner: arrive(sub, q, owner))
        for owner in range(n_col):
            high, low = split(col[sub, owner])
            at = owner * width
            b_cat[sub, :, at:at + width] = high
            b_cat[sub, :, depth + at:depth + at + width] = low
            b_cat[sub, :, 2 * depth + at:2 * depth + at + width] = high

    def multiply(sub, part):
        into = snd if part == 0 else mine_ref
        for t in range(tiles):
            product = lax.dot_general(
                a_cat[part * keep:(part + 1) * keep, :], b_cat[sub, t * tile:(t + 1) * tile, :],
                (((1,), (1,)), ((), ())), preferred_element_type=F32,
            )
            for b in range(2):
                q = t * 2 + b
                column = (q * subs + sub) * BLK
                into[sub * n_row + q] = (
                    front_sorted[part * keep:(part + 1) * keep, column:column + BLK]
                    - product[:, b * BLK:(b + 1) * BLK]
                )

    def send_sibling(sub):
        for t in range(tiles):
            sibling(sub, t).start()

    def sibling(sub, t):
        blocks = pl.ds(sub * n_row + t * 2, 2)
        return remote(
            snd.at[blocks], got_ref.at[blocks], sib_send.at[sub, t], sib_recv.at[sub, t], other_leaf=sib
        )

    sort_front()
    for sub in range(subs):
        gather(sub)
        if sub == 0:
            build_window(0)
        build_columns(sub)
        multiply(sub, 0)
        send_sibling(sub)
    relay_window(1)
    build_window(1)
    for sub in range(subs):
        multiply(sub, 1)

    for sub in range(subs):
        for t in range(tiles):
            sibling(sub, t).wait()
    to_relay.wait_send()
    for part in range(2):
        for side in range(2):
            @pl.when(has(side))
            def _():
                pass_window(part, c, side).wait_send()

            for d in range(1, n_col - 1):
                owner = c - d if side == 0 else c + d

                @pl.when(jnp.logical_and(from_left(d) if side == 0 else from_right(d), has(side)))
                def _():
                    pass_window(part, owner, side).wait_send()
    for sub in range(subs):
        for own in (True, False):
            for kk in range(2):
                here, away, stay = scatter(sub, own, kk)

                @pl.when(jnp.logical_not(here))
                def _():
                    away.wait_send()
        for offset in steps:
            def settle(owner):
                hand_on(sub, r, owner, s2_send.at[sub, owner, 0], x_row).wait_send()
                hand_on(sub, r, owner, s2_send.at[sub, owner, 1], pair_row).wait_send()
                hand_on(sub, x_row, owner, fwd_send.at[sub, owner], pair_row).wait_send()

            each(offset, settle)


def merge_kernel(n_row, subs, blocks, own_ref, other_ref, mine_hbm, got_hbm, out_ref, got_ref, mine_sem, got_sem):
    def at(j):
        return (j % subs) * n_row + j // subs

    def spot(maps, j):
        return pl.ds(pl.multiple_of(maps[0, j] * BLK, BLK), BLK)

    def bring(j):
        return pltpu.make_async_copy(got_hbm.at[at(j)], got_ref.at[j], got_sem.at[j])

    def lay(j):
        return pltpu.make_async_copy(mine_hbm.at[at(j)], out_ref.at[:, spot(own_ref, j)], mine_sem.at[j])

    for j in range(blocks):
        lay(j).start()
    for j in range(blocks):
        bring(j).start()
    for j in range(blocks, out_ref.shape[1] // BLK):
        out_ref[:, spot(own_ref, j)] = jnp.zeros((out_ref.shape[0], BLK), F32)
    for j in range(blocks):
        lay(j).wait()
    for j in range(blocks):
        bring(j).wait()
        out_ref[:, spot(other_ref, j)] = out_ref[:, spot(other_ref, j)] + got_ref[j]


def body(sizes, panel, block_mask, front_rest, row_maps, col_maps):
    n_leaf, n_row, n_col = sizes
    local_rows, width = panel.shape
    win_rows, front_cols = front_rest.shape
    keep = win_rows // 2
    blocks = front_cols // BLK
    subs = local_rows // n_row // BLK
    parent_cols = PC // n_col
    pairs = [(source, source ^ (n_leaf // 2)) for source in range(n_leaf)]
    other_cols = lax.ppermute(col_maps, "leaf", pairs)
    flags = block_mask.astype(F32)
    masked = (
        panel.reshape(local_rows // BLK, BLK, width // BLK, BLK) * flags[:, None, :, None]
    ).reshape(local_rows, width)
    win_blocks = win_rows // BLK
    pick = (row_maps == jnp.arange(win_blocks, dtype=row_maps.dtype)[:, None]).astype(F32)
    pick = jnp.broadcast_to(pick.reshape(-1, 1, 1), (win_blocks * win_blocks, 1, front_cols))
    vmem = pl.BlockSpec(memory_space=pltpu.VMEM)
    smem = pl.BlockSpec(memory_space=pltpu.SMEM)
    dma = pltpu.SemaphoreType.DMA
    part = jax.ShapeDtypeStruct((blocks, keep, BLK), F32)
    mine, got = pl.pallas_call(
        functools.partial(update_kernel, n_leaf, n_row, n_col),
        out_shape=(part, part),
        in_specs=[vmem, vmem, pl.BlockSpec(memory_space=pl.ANY)],
        out_specs=(vmem, vmem),
        scratch_shapes=[
            pltpu.VMEM((local_rows // 2, width), F32),
            pltpu.VMEM((2, n_col, keep, width), F32),
            pltpu.VMEM((subs, n_col, n_row * BLK, width), F32),
            pltpu.VMEM((win_rows, 3 * n_col * width), BF16),
            pltpu.VMEM((subs, n_row * BLK, 3 * n_col * width), BF16),
            pltpu.VMEM((win_rows, front_cols), F32),
            pltpu.VMEM((win_rows, front_cols), F32),
            pltpu.VMEM((blocks, keep, BLK), F32),
            dma((2, 2, n_col)), dma((2, n_col)),
            dma((1,)), dma((1,)),
            dma((subs, 2, 2)), dma((subs, n_row, n_col)),
            dma((subs, n_col, 2)), dma((subs, n_col)),
            dma((subs, n_row // 2)), dma((subs, n_row // 2)),
            dma((1,)), dma((subs,)),
        ],
        compiler_params=pltpu.CompilerParams(
            collective_id=0, has_side_effects=True, vmem_limit_bytes=40 * 1024 * 1024
        ),
        name="update",
    )(pick, masked, front_rest)
    return pl.pallas_call(
        functools.partial(merge_kernel, n_row, subs, blocks),
        out_shape=jax.ShapeDtypeStruct((keep, parent_cols), F32),
        in_specs=[smem, smem] + [pl.BlockSpec(memory_space=pl.ANY)] * 2,
        out_specs=vmem,
        scratch_shapes=[pltpu.VMEM((blocks, keep, BLK), F32), dma((blocks,)), dma((blocks,))],
        name="merge",
    )(col_maps, other_cols, mine, got)


def solution(mesh):
    sizes = mesh.shape["leaf"], mesh.shape["row"], mesh.shape["col"]
    return jax.shard_map(
        functools.partial(body, sizes),
        mesh=mesh,
        in_specs=(
            P(("leaf", "row"), "col"),
            P(("leaf", "row"), "col"),
            P(("leaf", "row"), "col"),
            P(("leaf", "row"), None),
            P(("leaf", "col"), None),
        ),
        out_specs=P(("leaf", "row"), "col"),
        check_vma=False,
    )
```

```python
import functools

import jax
import jax.numpy as jnp
from jax import lax
from jax.experimental import pallas as pl
from jax.experimental.pallas import tpu as pltpu
from jax.sharding import PartitionSpec as P

BLK = 128
PC = 6144
F32 = jnp.float32
BF16 = jnp.bfloat16


def split(value):
    high = value.astype(BF16)
    return high, (value - high.astype(F32)).astype(BF16)


def update_kernel(
    n_leaf, n_row, n_col,
    pick_ref, flag_ref, cols_ref, panel_ref, front_hbm,
    mine_ref, got_ref, other_ref,
    p_ref, relay, win, col, a_cat, b_cat, front, front_sorted, snd,
    win_send, win_recv, rel_send, rel_recv, s1_send, col_recv, s2_send, fwd_send,
    sib_send, sib_recv, loc_sem, self_sem, map_send, map_recv,
):
    leaf, r, c = lax.axis_index("leaf"), lax.axis_index("row"), lax.axis_index("col")
    x, k = r // 2, r % 2
    sib = lax.rem(leaf + n_leaf // 2, n_leaf)
    upper = leaf // (n_leaf // 2) % 2
    keep, width = win.shape[2], win.shape[3]
    win_rows = 2 * keep
    win_blocks = win_rows // BLK
    subs = col.shape[0]
    quarter = p_ref.shape[0] // n_row
    depth = n_col * width

    def remote(src, dst, ssem, rsem, row=None, column=None, other_leaf=None):
        where = {
            "leaf": leaf if other_leaf is None else other_leaf,
            "row": r if row is None else row,
            "col": c if column is None else column,
        }
        return pltpu.make_async_remote_copy(
            src_ref=src, dst_ref=dst, send_sem=ssem, recv_sem=rsem,
            device_id=where, device_id_type=pl.DeviceIdType.MESH,
        )

    x_row, pair_row = (1 - x) * 2 + k, x * 2 + 1 - k

    front_copy = pltpu.make_async_copy(front_hbm, front, loc_sem.at[0])
    front_copy.start()
    first_kept = upper * (win_blocks // 2)
    first_sent = (1 - upper) * (win_blocks // 2)
    parent_at = [first_sent + i for i in range(win_blocks // 2)]
    parent_at += [first_kept + i for i in range(win_blocks // 2)]

    def picked(block_of, index, lanes):
        total = None
        for j in range(win_blocks):
            term = block_of(j) * pick_ref[parent_at[index] * win_blocks + j][:, :lanes]
            total = term if total is None else total + term
        return total

    for i in range(p_ref.shape[0] // BLK):
        for b in range(p_ref.shape[1] // BLK):
            spot = slice(i * BLK, (i + 1) * BLK), slice(b * BLK, (b + 1) * BLK)
            flag = flag_ref[i:i + 1, b:b + 1].astype(F32)
            p_ref[spot] = panel_ref[spot] * jnp.broadcast_to(flag, (BLK, BLK))

    for i in range(win_blocks):
        win[i * BLK // keep, c, pl.ds(i * BLK % keep, BLK), :] = picked(
            lambda j: p_ref[j * BLK:(j + 1) * BLK, :], i, p_ref.shape[1]
        )

    barrier = pltpu.get_barrier_semaphore()

    def greet(row, column, other_leaf):
        pl.semaphore_signal(
            barrier, inc=1, device_id={"leaf": other_leaf, "row": row, "col": column},
            device_id_type=pl.DeviceIdType.MESH,
        )

    for step in range(1, n_col):
        for kk in range(2):
            greet(x * 2 + kk, lax.rem(c + step, n_col), leaf)
    greet(pair_row, c, leaf)
    greet(x_row, c, leaf)
    greet(r, c, sib)
    pl.semaphore_wait(barrier, 2 * (n_col - 1) + 3)

    def pass_window(part, owner, side):
        piece = win.at[part, owner]
        return remote(
            piece, piece, win_send.at[part, side, owner], win_recv.at[part, owner],
            column=c + 1 if side == 0 else c - 1,
        )

    def has(side):
        return c + 1 < n_col if side == 0 else c >= 1

    def send_window(part):
        for side in range(2):
            @pl.when(has(side))
            def _():
                pass_window(part, c, side).start()

    other_cols = remote(cols_ref, other_ref, map_send.at[0], map_recv.at[0], other_leaf=sib)
    other_cols.start()
    send_window(0)
    half = 2 * quarter
    to_relay = remote(
        p_ref.at[pl.ds(pl.multiple_of((1 - x) * half, half), half)], relay,
        rel_send.at[0], rel_recv.at[0], row=x_row,
    )
    to_relay.start()

    def from_left(d):
        return c - d >= 0

    def from_right(d):
        return c + d < n_col

    def take_window(part, d, side, forward):
        owner = c - d if side == 0 else c + d

        @pl.when(from_left(d) if side == 0 else from_right(d))
        def _():
            pass_window(part, owner, side).wait_recv()
            if forward:
                @pl.when(has(side))
                def _():
                    pass_window(part, owner, side).start()

    def relay_window(part):
        for d in range(1, n_col - 1):
            for side in range(2):
                take_window(part, d, side, True)

    relay_window(0)

    to_relay.wait_recv()

    def scatter(sub, own, kk):
        target = x * 2 + k if own else (1 - x) * 2 + k
        q = x * 2 + kk
        if own:
            start = pl.multiple_of(q * quarter + sub * BLK, BLK)
            src = p_ref.at[pl.ds(start, BLK)]
        else:
            src = relay.at[pl.ds(kk * quarter + sub * BLK, BLK)]
        dst = col.at[sub, c, pl.ds(pl.multiple_of(q * BLK, BLK), BLK)]
        slot = s1_send.at[sub, int(own), kk]
        here = jnp.logical_and(target == c, k == kk)
        away = remote(src, dst, slot, col_recv.at[sub, q, c], row=q, column=target)
        stay = pltpu.make_async_copy(src, dst, self_sem.at[sub])
        return here, away, stay

    def at_end(own):
        target = x * 2 + k if own else (1 - x) * 2 + k
        return jnp.logical_or(target == 0, target == n_col - 1)

    def send_quarters(sub, own, kk):
        here, away, stay = scatter(sub, own, kk)

        @pl.when(here)
        def _():
            stay.start()

        @pl.when(jnp.logical_not(here))
        def _():
            away.start()

    for sub in range(subs):
        for last in (True, False):
            for own in (True, False):
                @pl.when(at_end(own) if last else jnp.logical_not(at_end(own)))
                def _():
                    for kk in range(2):
                        send_quarters(sub, own, kk)

    send_window(1)

    def slot_of(sub, q, owner):
        return col.at[sub, owner, pl.ds(pl.multiple_of(q * BLK, BLK), BLK)]

    def hand_on(sub, q, owner, ssem, row):
        part = slot_of(sub, q, owner)
        return remote(part, part, ssem, col_recv.at[sub, q, owner], row=row)

    steps = [0]
    for d in range(1, n_col):
        steps += [-d, d]

    def each(offset, run):
        owner = c + offset
        if offset == 0:
            run(owner)
        else:
            @pl.when(from_left(-offset) if offset < 0 else from_right(offset))
            def _():
                run(owner)

    def arrive(sub, q, owner):
        hand_on(sub, q, owner, s2_send.at[sub, owner, 0], pair_row).wait_recv()

    is_source = k == c % 2

    def own_piece_at(sub, offset):
        def run(owner):
            if offset == 0:
                @pl.when(is_source)
                def _():
                    pltpu.make_async_copy(
                        slot_of(sub, r, owner), slot_of(sub, r, owner), self_sem.at[sub]
                    ).wait()

                @pl.when(jnp.logical_not(is_source))
                def _():
                    arrive(sub, r, owner)
            else:
                arrive(sub, r, owner)
            hand_on(sub, r, owner, s2_send.at[sub, owner, 0], x_row).start()
            hand_on(sub, r, owner, s2_send.at[sub, owner, 1], pair_row).start()
        return run

    def forward_piece(sub):
        def run(owner):
            arrive(sub, x_row, owner)
            hand_on(sub, x_row, owner, fwd_send.at[sub, owner], pair_row).start()
        return run

    def gather(sub):
        for at, offset in enumerate(steps):
            each(offset, own_piece_at(sub, offset))
            if at:
                each(steps[at - 1], forward_piece(sub))
        each(steps[-1], forward_piece(sub))

    def sort_front():
        front_copy.wait()
        for i in range(win_blocks):
            front_sorted[i * BLK:(i + 1) * BLK, :] = picked(
                lambda j: front[j * BLK:(j + 1) * BLK, :], i, front.shape[1]
            )

    def build_window(part):
        for side in range(2):
            take_window(part, n_col - 1, side, False)
        for owner in range(n_col):
            high, low = split(win[part, owner])
            at = owner * width
            rows = slice(part * keep, (part + 1) * keep)
            a_cat[rows, at:at + width] = high
            a_cat[rows, depth + at:depth + at + width] = high
            a_cat[rows, 2 * depth + at:2 * depth + at + width] = low

    tile = 2 * BLK
    tiles = n_row * BLK // tile

    def build_columns(sub):
        for q in (pair_row, (1 - x) * 2 + 1 - k):
            for offset in steps:
                each(offset, lambda owner: arrive(sub, q, owner))
        for owner in range(n_col):
            high, low = split(col[sub, owner])
            at = owner * width
            b_cat[sub, :, at:at + width] = high
            b_cat[sub, :, depth + at:depth + at + width] = low
            b_cat[sub, :, 2 * depth + at:2 * depth + at + width] = high

    def multiply(sub, part):
        into = snd if part == 0 else mine_ref
        for t in range(tiles):
            product = lax.dot_general(
                a_cat[part * keep:(part + 1) * keep, :], b_cat[sub, t * tile:(t + 1) * tile, :],
                (((1,), (1,)), ((), ())), preferred_element_type=F32,
            )
            for b in range(2):
                q = t * 2 + b
                column = (q * subs + sub) * BLK
                into[sub * n_row + q] = (
                    front_sorted[part * keep:(part + 1) * keep, column:column + BLK]
                    - product[:, b * BLK:(b + 1) * BLK]
                )

    def send_sibling(sub):
        for t in range(tiles):
            sibling(sub, t).start()

    def sibling(sub, t):
        blocks = pl.ds(sub * n_row + t * 2, 2)
        return remote(
            snd.at[blocks], got_ref.at[blocks], sib_send.at[sub, t], sib_recv.at[sub, t], other_leaf=sib
        )

    sort_front()
    for sub in range(subs):
        gather(sub)
        if sub == 0:
            build_window(0)
        build_columns(sub)
        multiply(sub, 0)
        send_sibling(sub)
    relay_window(1)
    build_window(1)
    for sub in range(subs):
        multiply(sub, 1)

    for sub in range(subs):
        for t in range(tiles):
            sibling(sub, t).wait()
    other_cols.wait()
    to_relay.wait_send()
    for part in range(2):
        for side in range(2):
            @pl.when(has(side))
            def _():
                pass_window(part, c, side).wait_send()

            for d in range(1, n_col - 1):
                owner = c - d if side == 0 else c + d

                @pl.when(jnp.logical_and(from_left(d) if side == 0 else from_right(d), has(side)))
                def _():
                    pass_window(part, owner, side).wait_send()
    for sub in range(subs):
        for own in (True, False):
            for kk in range(2):
                here, away, stay = scatter(sub, own, kk)

                @pl.when(jnp.logical_not(here))
                def _():
                    away.wait_send()
        for offset in steps:
            def settle(owner):
                hand_on(sub, r, owner, s2_send.at[sub, owner, 0], x_row).wait_send()
                hand_on(sub, r, owner, s2_send.at[sub, owner, 1], pair_row).wait_send()
                hand_on(sub, x_row, owner, fwd_send.at[sub, owner], pair_row).wait_send()

            each(offset, settle)


def merge_kernel(n_row, subs, blocks, own_ref, other_ref, mine_hbm, got_hbm, out_ref, got_ref, mine_sem, got_sem):
    def at(j):
        return (j % subs) * n_row + j // subs

    def spot(maps, j):
        return pl.ds(pl.multiple_of(maps[0, j] * BLK, BLK), BLK)

    def bring(j):
        return pltpu.make_async_copy(got_hbm.at[at(j)], got_ref.at[j], got_sem.at[j])

    def lay(j):
        return pltpu.make_async_copy(mine_hbm.at[at(j)], out_ref.at[:, spot(own_ref, j)], mine_sem.at[j])

    for j in range(blocks):
        lay(j).start()
    for j in range(blocks):
        bring(j).start()
    for j in range(blocks, out_ref.shape[1] // BLK):
        out_ref[:, spot(own_ref, j)] = jnp.zeros((out_ref.shape[0], BLK), F32)
    for j in range(blocks):
        lay(j).wait()
    for j in range(blocks):
        bring(j).wait()
        out_ref[:, spot(other_ref, j)] = out_ref[:, spot(other_ref, j)] + got_ref[j]


def body(sizes, panel, block_mask, front_rest, row_maps, col_maps):
    n_leaf, n_row, n_col = sizes
    local_rows, width = panel.shape
    win_rows, front_cols = front_rest.shape
    keep = win_rows // 2
    blocks = front_cols // BLK
    subs = local_rows // n_row // BLK
    parent_cols = PC // n_col
    win_blocks = win_rows // BLK
    pick = (row_maps == jnp.arange(win_blocks, dtype=row_maps.dtype)[:, None]).astype(F32)
    pick = jnp.broadcast_to(pick.reshape(-1, 1, 1), (win_blocks * win_blocks, 1, front_cols))
    vmem = pl.BlockSpec(memory_space=pltpu.VMEM)
    smem = pl.BlockSpec(memory_space=pltpu.SMEM)
    dma = pltpu.SemaphoreType.DMA
    part = jax.ShapeDtypeStruct((blocks, keep, BLK), F32)
    mine, got, other_cols = pl.pallas_call(
        functools.partial(update_kernel, n_leaf, n_row, n_col),
        out_shape=(part, part, jax.ShapeDtypeStruct(col_maps.shape, col_maps.dtype)),
        in_specs=[vmem] * 4 + [pl.BlockSpec(memory_space=pltpu.HBM)],
        out_specs=(vmem, vmem, vmem),
        scratch_shapes=[
            pltpu.VMEM((local_rows, width), F32),
            pltpu.VMEM((local_rows // 2, width), F32),
            pltpu.VMEM((2, n_col, keep, width), F32),
            pltpu.VMEM((subs, n_col, n_row * BLK, width), F32),
            pltpu.VMEM((win_rows, 3 * n_col * width), BF16),
            pltpu.VMEM((subs, n_row * BLK, 3 * n_col * width), BF16),
            pltpu.VMEM((win_rows, front_cols), F32),
            pltpu.VMEM((win_rows, front_cols), F32),
            pltpu.VMEM((blocks, keep, BLK), F32),
            dma((2, 2, n_col)), dma((2, n_col)),
            dma((1,)), dma((1,)),
            dma((subs, 2, 2)), dma((subs, n_row, n_col)),
            dma((subs, n_col, 2)), dma((subs, n_col)),
            dma((subs, n_row // 2)), dma((subs, n_row // 2)),
            dma((1,)), dma((subs,)), dma((1,)), dma((1,)),
        ],
        compiler_params=pltpu.CompilerParams(
            collective_id=0, has_side_effects=True, vmem_limit_bytes=40 * 1024 * 1024
        ),
        name="update",
    )(pick, block_mask, col_maps, panel, front_rest)
    return pl.pallas_call(
        functools.partial(merge_kernel, n_row, subs, blocks),
        out_shape=jax.ShapeDtypeStruct((keep, parent_cols), F32),
        in_specs=[smem, smem] + [pl.BlockSpec(memory_space=pl.ANY)] * 2,
        out_specs=vmem,
        scratch_shapes=[pltpu.VMEM((blocks, keep, BLK), F32), dma((blocks,)), dma((blocks,))],
        compiler_params=pltpu.CompilerParams(vmem_limit_bytes=8 * 1024 * 1024),
        name="merge",
    )(col_maps, other_cols, mine, got)


def solution(mesh):
    sizes = mesh.shape["leaf"], mesh.shape["row"], mesh.shape["col"]
    return jax.shard_map(
        functools.partial(body, sizes),
        mesh=mesh,
        in_specs=(
            P(("leaf", "row"), "col"),
            P(("leaf", "row"), "col"),
            P(("leaf", "row"), "col"),
            P(("leaf", "row"), None),
            P(("leaf", "col"), None),
        ),
        out_specs=P(("leaf", "row"), "col"),
        check_vma=False,
    )
```
